32 devices in a mesh: grp: 1, col: 32 (over z, y, x, core).
Axes of the slice: x: 2, y: 2, z: 4, core: 2. Of those that a mesh axis runs over, the one named last changes fastest.
Arguments:
- pair: bfloat16 [16, 1024, 128], P('grp', 'col'), may hold values from -6 to 6
- w_query: bfloat16 [128, 128], replicated, may hold values from -0.5 to 0.5
- w_kv: bfloat16 [128, 256], replicated, may hold values from -0.5 to 0.5
- w_gate: bfloat16 [128, 128], replicated, may hold values from -0.5 to 0.5
- w_out: bfloat16 [128, 128], replicated, may hold values from -0.5 to 0.5
- pair_bias: bfloat16 [4, 1024, 1024], P('grp', 'col'), may hold values from -8 to 300
- lengths: int32 [1], P('grp'), may hold values from 512 to 1024
Outputs:
- update: bfloat16 [16, 1024, 128], P('grp', 'col')
The draws below stay inside these ranges and needn't reach their ends.
All inputs are finite; a program needn't handle non-finite values.
Results may differ from the reference program's by a relative error of at most 0.0081.
Values may be sent and summed in bfloat16 or wider, within the bound.
No kernel may reach another device: no remote copies, remote signals or barrier semaphores. Data moves between devices by JAX's collectives and lax.ppermute only.
A program may use at most 128 MiB of HBM per device.

```python
import jax
import jax.numpy as jnp
from jax import lax

CHANNELS = 128
HEADS = 4
ROWS = 16
N_TOK = 1024


def draw_pair_bias(key, part):
    base = jnp.clip(2.0 * jax.random.normal(key, (HEADS, N_TOK, N_TOK), jnp.float32), -8.0, 8.0)
    return base.astype(jnp.bfloat16)


def block_scale(stream_key, dims, cuts, smallest, top_value):
    def one(axis_at, blocks):
        heights = jax.random.uniform(jax.random.fold_in(jax.random.fold_in(stream_key, 6), axis_at), (blocks,), jnp.float32, smallest / len(cuts), top_value / len(cuts))
        return jnp.repeat(jnp.exp(heights), dims[axis_at] // blocks).reshape((-1,) + (1,) * (len(dims) - axis_at - 1))

    loudness = one(*cuts[0])
    for cut in cuts[1:]:
        loudness = loudness * one(*cut)
    return loudness


def normal_values(key, dims, deviation, reach, split=(), kind=jnp.bfloat16):
    result = deviation * jax.random.normal(key, dims, jnp.float32)
    if split:
        result = result * block_scale(key, dims, split, -0.22, 0.18)
    return jnp.clip(result, -reach, reach).astype(kind)


def setup_inputs(seed: int = 0, part: int = 0) -> dict:
    key_of = jax.random.split(jax.random.key(seed), 8)
    part_splits = jax.random.split(jax.random.fold_in(key_of[7], part), 8)
    pair = normal_values(part_splits[0], (ROWS, N_TOK, CHANNELS), 1.0, 6.0, ((1, 32),))
    w_query = normal_values(key_of[1], (CHANNELS, CHANNELS), CHANNELS ** -0.5, 0.5)
    w_kv = normal_values(key_of[2], (CHANNELS, 2 * CHANNELS), CHANNELS ** -0.5, 0.5)
    w_gate = normal_values(key_of[3], (CHANNELS, CHANNELS), CHANNELS ** -0.5, 0.5)
    w_out = normal_values(key_of[4], (CHANNELS, CHANNELS), CHANNELS ** -0.5, 0.5)
    pair_bias = draw_pair_bias(jax.random.fold_in(jax.random.fold_in(key_of[7], part), 71), part)
    lengths = jax.random.randint(part_splits[6], (1,), N_TOK // 2, N_TOK + 1).astype(jnp.int32)
    return {"pair": pair, "w_query": w_query, "w_kv": w_kv, "w_gate": w_gate, "w_out": w_out, "pair_bias": pair_bias, "lengths": lengths}


def normalize(pair_row):
    values_f = pair_row.astype(jnp.float32)
    mean_val = lax.optimization_barrier(jnp.mean(values_f, axis=-1, keepdims=True))
    centred = values_f - mean_val
    variance = lax.optimization_barrier(jnp.mean(centred * centred, axis=-1, keepdims=True))
    return (centred * lax.rsqrt(variance + 1e-05)).astype(jnp.bfloat16)

def reference(pair, w_query, w_kv, w_gate, w_out, pair_bias, lengths):
    chan_count = pair.shape[-1]
    head_width = chan_count // HEADS
    bias_query = jnp.swapaxes(pair_bias, 1, 2).astype(jnp.float32)
    key_mask = jnp.where(jnp.arange(N_TOK) < lengths[0], 0.0, -1000000000.0).astype(jnp.float32)

    def one_row(pair_row):
        normed = normalize(pair_row)
        queries = (jnp.dot(normed, w_query, preferred_element_type=jnp.float32) * head_width ** (-0.5)).astype(jnp.bfloat16)
        queries = queries.reshape(N_TOK, HEADS, head_width)
        key_value = jnp.dot(normed, w_kv, preferred_element_type=jnp.float32).astype(jnp.bfloat16)
        key_tile = key_value[:, :chan_count].reshape(N_TOK, HEADS, head_width)
        value_tile = key_value[:, chan_count:].reshape(N_TOK, HEADS, head_width)
        gate_act = jax.nn.sigmoid(jnp.dot(normed, w_gate, preferred_element_type=jnp.float32))
        scores = jnp.einsum('jhd,khd->hjk', queries.astype(jnp.float32), key_tile.astype(jnp.float32))
        scores = scores + bias_query + key_mask
        row_max = lax.optimization_barrier(jnp.max(scores, axis=-1, keepdims=True))
        expon = jnp.exp(scores - row_max)
        total = lax.optimization_barrier(jnp.sum(expon, axis=-1))
        rounded = lax.optimization_barrier(expon.astype(jnp.bfloat16)).astype(jnp.float32)
        numer = jnp.einsum('hjk,khd->jhd', rounded, value_tile.astype(jnp.float32))
        attended = numer / jnp.transpose(total)[:, :, None]
        hidden = (gate_act * attended.reshape(N_TOK, chan_count)).astype(jnp.bfloat16)
        return jnp.dot(hidden, w_out, preferred_element_type=jnp.float32).astype(jnp.bfloat16)
    return lax.map(one_row, pair)
```

```python
import functools

import jax
import jax.numpy as jnp
from jax import lax
from jax.experimental import pallas as pl
from jax.experimental.pallas import tpu as pltpu
from jax.sharding import PartitionSpec as P

HEADS = 4
F32 = jnp.float32
BF16 = jnp.bfloat16
SMEM = pl.BlockSpec(memory_space=pltpu.SMEM)


def contract_last(a, b):
    return lax.dot_general(a, b, (((1,), (1,)), ((), ())), preferred_element_type=F32)


def normalized(values):
    values_f = values.astype(F32)
    mean_val = jnp.mean(values_f, axis=-1, keepdims=True)
    centred = values_f - mean_val
    variance = jnp.mean(centred * centred, axis=-1, keepdims=True)
    return (centred * lax.rsqrt(variance + 1e-05)).astype(BF16)


def norm_kernel(place, pair_ref, other_ref, block_ref):
    half_rows, width, _ = other_ref.shape
    core = place[1]
    own_at = pl.multiple_of(core * width, width)
    other_at = pl.multiple_of((1 - core) * width, width)
    block_ref[:, pl.ds(own_at, width), :] = normalized(pair_ref[pl.ds(core * half_rows, half_rows)])
    block_ref[:, pl.ds(other_at, width), :] = normalized(other_ref[...])


def query_kernel(block_ref, w_query_ref, w_kv_ref, w_gate_ref, query_ref, gate_ref):
    rows, cols, chans = block_ref.shape
    head_width = chans // HEADS
    tokens = block_ref[...].reshape(rows * cols, chans)
    queries = (
        jnp.dot(tokens, w_query_ref[...], preferred_element_type=F32) * head_width ** (-0.5)
    ).astype(BF16)
    lane_head = lax.broadcasted_iota(jnp.int32, queries.shape, 1) // head_width
    w_key = w_kv_ref[:, :chans]
    for head in range(HEADS):
        masked = jnp.where(lane_head == head, queries, jnp.zeros_like(queries))
        back = contract_last(masked, w_key).astype(BF16)
        query_ref[:, head * cols : (head + 1) * cols, :] = back.reshape(rows, cols, chans)
    gate = jax.nn.sigmoid(jnp.dot(tokens, w_gate_ref[...], preferred_element_type=F32))
    gate_ref[...] = gate.reshape(rows, cols, chans)


def pack_kernel(bias_ref, packed_ref):
    chips, width, lanes = packed_ref.shape
    cols = lanes // HEADS
    for chip in range(chips):
        for head in range(HEADS):
            packed_ref[chip, :, head * cols : (head + 1) * cols] = bias_ref[
                head, :, chip * cols : (chip + 1) * cols
            ]


def bias_kernel(offsets, place, own_ref, other_ref, bias_ref, keys_ref):
    width, lanes = own_ref.shape[1:]
    chip, core, limit = place[0], place[1], place[2]
    steps = (0, 1 + core, 2 - core, 3)
    row_at = lax.broadcasted_iota(jnp.int32, (width, lanes), 0)
    for spot, (far, near) in enumerate(offsets):
        source = chip ^ far ^ steps[near]
        for part_ref, part in ((own_ref, core), (other_ref, 1 - core)):
            first_key = (source * 2 + part) * width
            mask = jnp.where(first_key + row_at < limit, 0.0, -1000000000.0).astype(F32)
            at = pl.multiple_of(spot * 2 * width + part * width, width)
            keys_ref[pl.ds(at, width), :] = part_ref[source].astype(F32) + mask
    bias_ref[...] = keys_ref[...].T


def attend_kernel(place, *refs):
    pieces = refs[:8]
    query_ref, bias_ref, gate_ref, w_kv_ref, w_out_ref, keep_ref, send_ref, out_ref = refs[8:]
    width, chans = keep_ref.shape[1:]
    cols = 2 * width
    head_width = chans // HEADS
    keys = jnp.concatenate([piece[...].reshape(-1, chans) for piece in pieces], axis=0)
    scores = contract_last(query_ref[0], keys) + bias_ref[...]
    top = jnp.max(scores, axis=-1, keepdims=True)
    expon = jnp.exp(scores - top)
    total = jnp.sum(expon, axis=-1, keepdims=True)
    mixed = jnp.dot(expon.astype(BF16), keys, preferred_element_type=F32)
    mixed = (mixed / total).astype(BF16)
    w_value = w_kv_ref[:, chans:]
    lane_head = lax.broadcasted_iota(jnp.int32, (cols, chans), 1) // head_width
    attended = jnp.zeros((cols, chans), F32)
    for head in range(HEADS):
        one = jnp.dot(mixed[head * cols : (head + 1) * cols], w_value, preferred_element_type=F32)
        attended = jnp.where(lane_head == head, one, attended)
    hidden = (gate_ref[0] * attended).astype(BF16)
    out_ref[...] = jnp.dot(hidden, w_out_ref[...], preferred_element_type=F32).astype(BF16)
    core = place[1]
    keep_ref[0] = out_ref[pl.ds(pl.multiple_of(core * width, width), width), :]
    send_ref[0] = out_ref[pl.ds(pl.multiple_of((1 - core) * width, width), width), :]


def join_kernel(place, keep_ref, recv_ref, out_ref):
    half_rows = keep_ref.shape[0]
    core = place[1]
    out_ref[pl.ds(core * half_rows, half_rows)] = keep_ref[...]
    out_ref[pl.ds((1 - core) * half_rows, half_rows)] = recv_ref[...]


def whole(count):
    return [pl.BlockSpec(memory_space=pltpu.VMEM)] * count


def on_device(n_dev, pair, w_query, w_kv, w_gate, w_out, pair_bias, lengths):
    rows, width, chans = pair.shape
    half_rows = rows // 2
    cols = 2 * width
    chips = n_dev // 2
    index = lax.axis_index("col")
    core = index % 2
    place = jnp.stack([index // 2, core, lengths[0]]).astype(jnp.int32)

    def swap(value, chip_xor):
        perm = [(d, ((d // 2) ^ chip_xor(d % 2)) * 2 + d % 2) for d in range(n_dev)]
        return lax.ppermute(value, "col", perm)

    def swap_core(value):
        return lax.ppermute(value, "col", [(d, d ^ 1) for d in range(n_dev)])

    other = swap_core(lax.dynamic_slice_in_dim(pair, (1 - core) * half_rows, half_rows, 0))

    packed = pl.pallas_call(
        pack_kernel,
        out_shape=jax.ShapeDtypeStruct((chips, width, HEADS * cols), BF16),
        name="pack_bias",
    )(pair_bias)

    block = pl.pallas_call(
        norm_kernel,
        in_specs=[SMEM] + whole(2),
        out_shape=jax.ShapeDtypeStruct((half_rows, cols, chans), BF16),
        name="norm",
    )(place, pair, other)

    near = block[None]
    far_offsets = [0]
    bit = 4
    while bit * 2 < chips:
        near = jnp.concatenate([near, swap(near, lambda c: bit)], axis=0)
        far_offsets = far_offsets + [f ^ bit for f in far_offsets]
        bit *= 2
    far = swap(near, lambda c: bit)
    far_twin = [f ^ bit for f in far_offsets]

    def spread(piece):
        first = swap(piece, lambda c: 1 + c)
        second = swap(piece, lambda c: 2 - c)
        third = swap(first, lambda c: 2 - c)
        return [piece, first, second, third]

    pieces = spread(near) + spread(far)
    offsets = [(f, s) for group in (far_offsets, far_twin) for s in range(4) for f in group]

    same_core = [[chip * 2 + c for chip in range(chips)] for c in range(2)]
    own_bias = lax.all_to_all(
        packed, "col", 0, 0, tiled=True, axis_index_groups=same_core
    )
    other_bias = swap_core(own_bias)

    query, gate = pl.pallas_call(
        query_kernel,
        out_shape=(
            jax.ShapeDtypeStruct((half_rows, HEADS * cols, chans), BF16),
            jax.ShapeDtypeStruct((half_rows, cols, chans), F32),
        ),
        name="query",
    )(block, w_query, w_kv, w_gate)

    n_keys = chips * cols
    bias = pl.pallas_call(
        functools.partial(bias_kernel, offsets),
        in_specs=[SMEM] + whole(2),
        out_shape=jax.ShapeDtypeStruct((HEADS * cols, n_keys), F32),
        scratch_shapes=[pltpu.VMEM((n_keys, HEADS * cols), F32)],
        name="bias",
    )(place, own_bias, other_bias)

    piece_spec = pl.BlockSpec((near.shape[0], 1, cols, chans), lambda r: (0, r, 0, 0))

    def row_spec(size):
        return pl.BlockSpec((1, size, chans), lambda r: (r, 0, 0))

    def full_spec(value):
        return pl.BlockSpec(value.shape, lambda r: (0,) * value.ndim)

    keep, send = pl.pallas_call(
        attend_kernel,
        grid=(half_rows,),
        in_specs=[SMEM]
        + [piece_spec] * 8
        + [row_spec(HEADS * cols), full_spec(bias), row_spec(cols), full_spec(w_kv), full_spec(w_out)],
        out_specs=[row_spec(width)] * 2,
        out_shape=[jax.ShapeDtypeStruct((half_rows, width, chans), BF16)] * 2,
        scratch_shapes=[pltpu.VMEM((cols, chans), BF16)],
        name="attend",
    )(place, *pieces, query, bias, gate, w_kv, w_out)

    return pl.pallas_call(
        join_kernel,
        in_specs=[SMEM] + whole(2),
        out_shape=jax.ShapeDtypeStruct(pair.shape, BF16),
        name="join",
    )(place, keep, swap_core(send))


def solution(mesh):
    in_specs = (P("grp", "col", None), P(), P(), P(), P(), P("grp", "col", None), P("grp"))
    out_specs = P("grp", "col", None)
    return jax.shard_map(
        functools.partial(on_device, mesh.shape["col"]),
        mesh=mesh,
        in_specs=in_specs,
        out_specs=out_specs,
        check_vma=False,
    )
```

```python
import functools
import math

import jax
import jax.numpy as jnp
from jax import lax
from jax.experimental import pallas as pl
from jax.experimental.pallas import tpu as pltpu
from jax.sharding import PartitionSpec as P


HEADS = 4
F32 = jnp.float32
BF16 = jnp.bfloat16
MIB = 1 << 20
LOG2_E = math.log2(math.e)


def vmem_call(kernel, outs, *args, plain=(), in_hbm=False, scratch=(), scalars=(), room=4 * MIB):
    args = [*plain, *(pltpu.with_memory_space_constraint(a, pltpu.VMEM) for a in args)]
    if in_hbm:
        out_shape = [jax.ShapeDtypeStruct(*o) for o in outs]
    else:
        out_shape = [pltpu.VMEM(*o) for o in outs]
    call = pl.pallas_call(
        kernel,
        in_specs=[pl.BlockSpec(memory_space=pltpu.SMEM)] * len(scalars)
        + [pl.BlockSpec(memory_space=pltpu.VMEM)] * len(args),
        out_specs=[pl.BlockSpec(memory_space=pltpu.VMEM)] * len(outs),
        out_shape=out_shape,
        scratch_shapes=scratch,
        compiler_params=pltpu.CompilerParams(vmem_limit_bytes=room),
    )
    results = call(*scalars, *args)
    return results if len(outs) > 1 else results[0]


def my_place():
    index = lax.axis_index("col")
    return index >> 1, index & 1


def contract_last(a, b):
    return lax.dot_general(a, b, (((1,), (1,)), ((), ())), preferred_element_type=F32)


def normalized(values):
    values_f = values.astype(F32)
    mean_val = jnp.mean(values_f, axis=-1, keepdims=True)
    centred = values_f - mean_val
    variance = jnp.mean(centred * centred, axis=-1, keepdims=True)
    return (centred * lax.rsqrt(variance + 1e-05)).astype(BF16)


def early_kernel(stages, pair_ref, bias_ref, own_ref, keep_ref, send_ref, packed_ref):
    half_rows = own_ref.shape[0]
    _, core = my_place()
    own_ref[...] = normalized(pair_ref[pl.ds(core * half_rows, half_rows)])
    pack_bias(stages, bias_ref, keep_ref, send_ref, packed_ref)


def norm_kernel(own_ref, other_ref, block_ref):
    half_rows, width, _ = own_ref.shape
    _, core = my_place()
    own_at = pl.multiple_of(core * width, width)
    other_at = pl.multiple_of((1 - core) * width, width)
    block_ref[0, :, pl.ds(own_at, width), :] = own_ref[...]
    block_ref[0, :, pl.ds(other_at, width), :] = normalized(
        other_ref[pl.ds(core * half_rows, half_rows)]
    )


def stack_kernel(first_ref, second_ref, out_ref):
    count = first_ref.shape[0]
    out_ref[:count] = first_ref[...]
    out_ref[count:] = second_ref[...]


def query_kernel(block_ref, w_query_ref, w_kv_ref, w_gate_ref, query_ref, gate_ref):
    _, rows, cols, chans = block_ref.shape
    head_width = chans // HEADS
    tokens = block_ref[...].reshape(rows * cols, chans)
    queries = (
        jnp.dot(tokens, w_query_ref[...], preferred_element_type=F32) * head_width ** (-0.5)
    ).astype(BF16)
    lane_head = lax.broadcasted_iota(jnp.int32, queries.shape, 1) // head_width
    w_key = w_kv_ref[:, :chans]
    for head in range(HEADS):
        masked = jnp.where(lane_head == head, queries, jnp.zeros_like(queries))
        back = (contract_last(masked, w_key) * LOG2_E).astype(BF16)
        query_ref[:, head * cols : (head + 1) * cols, :] = back.reshape(rows, cols, chans)
    gate = jax.nn.sigmoid(jnp.dot(tokens, w_gate_ref[...], preferred_element_type=F32))
    gate_ref[...] = gate.reshape(rows, cols, chans)


def pack_bias(stages, bias_ref, keep_ref, send_ref, packed_ref):
    half = keep_ref.shape[1]
    chips, _, lanes = packed_ref.shape
    cols = lanes // HEADS
    chip, core = my_place()
    for target in range(chips):
        apart = chip ^ target
        spot = 0
        for stage in stages:
            shift = {"first": core, "second": 1 - core}.get(stage)
            if shift is None:
                shift = stage.bit_length() - 1
            spot = spot * 2 + ((apart >> shift) & 1)
        for head in range(HEADS):
            packed_ref[spot, :, head * cols : (head + 1) * cols] = bias_ref[
                head, :, target * cols : (target + 1) * cols
            ]
    keep_ref[0] = packed_ref[:half]
    send_ref[0] = packed_ref[half:]


def trade_kernel(keep_ref, recv_ref, next_keep_ref, next_send_ref):
    sources, targets = keep_ref.shape[:2]
    half = targets // 2
    next_keep_ref[:sources] = keep_ref[:, :half]
    next_keep_ref[sources:] = recv_ref[:, :half]
    next_send_ref[:sources] = keep_ref[:, half:]
    next_send_ref[sources:] = recv_ref[:, half:]


def bias_kernel(offsets, spots, limit_ref, own_a, own_b, other_a, other_b, bias_ref, keys_ref):
    sources, _, width, lanes = own_a.shape
    chip, core = my_place()
    limit = limit_ref[0]
    steps = (0, 1 + core, 2 - core, 3)
    flipped = (0, 2, 1, 3)
    row_at = lax.broadcasted_iota(jnp.int32, (width, lanes), 0)
    for spot, (far, near) in enumerate(offsets):
        source = chip ^ far ^ steps[near]
        for parts, part, seen in (
            ((own_a, own_b), core, near),
            ((other_a, other_b), 1 - core, flipped[near]),
        ):
            first_key = (source * 2 + part) * width
            mask = jnp.where(first_key + row_at < limit, 0.0, -1000000000.0).astype(F32)
            at = pl.multiple_of(spot * 2 * width + part * width, width)
            held = spots[far, seen]
            value = parts[held // sources][held % sources, 0]
            keys_ref[pl.ds(at, width), :] = (value.astype(F32) + mask) * LOG2_E
    bias_ref[...] = keys_ref[...].T


def attend_rows(key_at, pieces, query_ref, bias_ref, finish):
    rows, lanes, chans = query_ref.shape
    n_keys = sum(piece.shape[0] * piece.shape[2] for piece in pieces)
    step = rows
    while step > 1 and step * lanes * n_keys * 4 > 4 * MIB:
        step //= 2

    def advance(turn, carry):
        at = [turn * step + inner for inner in range(step)]
        keys = [
            jnp.concatenate([piece[:, row].reshape(-1, chans) for piece in pieces], axis=0)
            for row in at
        ]
        bias = bias_ref[:, key_at : key_at + n_keys]
        scores = [contract_last(query_ref[row], key) + bias for row, key in zip(at, keys)]
        tops = [jnp.max(score, axis=-1, keepdims=True) for score in scores]
        expons = [jnp.exp2(score - top) for score, top in zip(scores, tops)]
        totals = [jnp.sum(expon, axis=-1, keepdims=True) for expon in expons]
        mixes = [
            jnp.dot(expon.astype(BF16), key, preferred_element_type=F32)
            for expon, key in zip(expons, keys)
        ]
        for values in zip(at, tops, totals, mixes):
            finish(*values)
        return carry

    if step == rows:
        advance(0, 0)
    else:
        lax.fori_loop(0, rows // step, advance, 0)


def near_kernel(*refs):
    pieces = refs[:4]
    query_ref, bias_ref, top_ref, total_ref, mixed_ref = refs[4:]

    def finish(row, top, total, mixed):
        top_ref[row] = jnp.broadcast_to(top, mixed.shape)
        total_ref[row] = jnp.broadcast_to(total, mixed.shape)
        mixed_ref[row] = mixed

    attend_rows(0, pieces, query_ref, bias_ref, finish)


def far_kernel(*refs):
    pieces = refs[:4]
    (query_ref, bias_ref, top_ref, total_ref, mixed_ref, gate_ref, w_kv_ref, w_out_ref) = refs[4:12]
    keep_ref, send_ref, ready_ref, out_ref = refs[12:]
    rows, cols, chans = gate_ref.shape
    width = keep_ref.shape[1]
    head_width = chans // HEADS
    half_keys = bias_ref.shape[1] // 2

    def finish(row, top, total, mixed):
        old_top = top_ref[row]
        new_top = jnp.maximum(old_top, top)
        old_scale = jnp.exp2(old_top - new_top)
        scale = jnp.exp2(top - new_top)
        inverse = 1.0 / (total_ref[row] * old_scale + total * scale)
        both = mixed_ref[row] * (old_scale * inverse) + mixed * (scale * inverse)
        both = both.astype(BF16)
        for head in range(HEADS):
            ready_ref[head, row] = both[head * cols : (head + 1) * cols]

    attend_rows(half_keys, pieces, query_ref, bias_ref, finish)

    w_value = w_kv_ref[:, chans:]
    lane_head = lax.broadcasted_iota(jnp.int32, w_value.shape, 1) // head_width
    values = [jnp.where(lane_head == h, w_value, jnp.zeros_like(w_value)) for h in range(HEADS)]
    ready = [ready_ref[h].reshape(rows * cols, chans) for h in range(HEADS)]
    attended = jnp.dot(
        jnp.concatenate(ready, axis=1), jnp.concatenate(values, axis=0), preferred_element_type=F32
    )
    hidden = (gate_ref[...].reshape(rows * cols, chans) * attended).astype(BF16)
    update = jnp.dot(hidden, w_out_ref[...], preferred_element_type=F32).astype(BF16)
    out_ref[...] = update.reshape(rows, cols, chans)
    _, core = my_place()
    keep_ref[...] = out_ref[:, pl.ds(pl.multiple_of(core * width, width), width), :]
    send_ref[...] = out_ref[:, pl.ds(pl.multiple_of((1 - core) * width, width), width), :]


def join_kernel(keep_ref, recv_ref, out_ref):
    half_rows = keep_ref.shape[0]
    _, core = my_place()
    out_ref[pl.ds(core * half_rows, half_rows)] = keep_ref[...]
    out_ref[pl.ds((1 - core) * half_rows, half_rows)] = recv_ref[...]


def on_device(n_dev, pair, w_query, w_kv, w_gate, w_out, pair_bias, lengths):
    rows, width, chans = pair.shape
    half_rows = rows // 2
    cols = 2 * width
    lanes = HEADS * cols
    chips = n_dev // 2

    def swap(value, stage):
        def partner(d):
            apart = {"first": 1 + d % 2, "second": 2 - d % 2}.get(stage, stage)
            return ((d // 2) ^ apart) * 2 + d % 2

        return lax.ppermute(value, "col", [(d, partner(d)) for d in range(n_dev)])

    def swap_core(value):
        return lax.ppermute(value, "col", [(d, d ^ 1) for d in range(n_dev)])

    def spread(piece):
        first = swap(piece, "first")
        second = swap(piece, "second")
        third = swap(first, "second")
        return [piece, first, second, third]

    far_bits, stages = travel(n_dev)

    other = swap_core(pair)
    half_targets = ((1, chips // 2, width, lanes), BF16)
    own, keep_bias, send_bias = vmem_call(
        functools.partial(early_kernel, stages),
        [((half_rows, width, chans), BF16), half_targets, half_targets],
        plain=[pair, pair_bias],
        scratch=[pltpu.VMEM((chips, width, lanes), BF16)],
        room=4 * MIB + 4 * chips * width * lanes,
    )
    near = vmem_call(norm_kernel, [((1, half_rows, cols, chans), BF16)], own, other)
    block = near

    near_offsets = [0]
    for bit in far_bits[:0:-1]:
        arrived = swap(near, bit)
        shape = (2 * near.shape[0],) + near.shape[1:]
        near = vmem_call(stack_kernel, [(shape, BF16)], near, arrived)
        near_offsets = near_offsets + [f ^ bit for f in near_offsets]
    far = swap(near, far_bits[0])
    far_offsets = [f ^ far_bits[0] for f in near_offsets]

    near_pieces = spread(near)
    far_pieces = spread(far)
    offsets = [(f, s) for group in (near_offsets, far_offsets) for s in range(4) for f in group]

    for stage in stages[:-1]:
        recv_bias = swap(send_bias, stage)
        sources, targets = keep_bias.shape[:2]
        shape = (2 * sources, targets // 2, width, lanes)
        keep_bias, send_bias = vmem_call(trade_kernel, [(shape, BF16)] * 2, keep_bias, recv_bias)
    recv_bias = swap(send_bias, stages[-1])
    spots = {}
    for held in range(chips):
        taken = [stage for k, stage in enumerate(stages) if held >> k & 1]
        near_step = ("first" in taken) + 2 * ("second" in taken)
        spots[sum(t for t in taken if not isinstance(t, str)), near_step] = held

    query, gate = vmem_call(
        query_kernel,
        [((half_rows, lanes, chans), BF16), ((half_rows, cols, chans), F32)],
        block, w_query, w_kv, w_gate,
    )
    n_keys = chips * cols
    bias = vmem_call(
        functools.partial(bias_kernel, offsets, spots),
        [((lanes, n_keys), F32)],
        keep_bias, recv_bias,
        swap_core(keep_bias), swap_core(recv_bias),
        scratch=[pltpu.VMEM((n_keys, lanes), F32)],
        scalars=[lengths],
        room=4 * MIB + 3 * n_keys * lanes * 4,
    )
    state = vmem_call(
        near_kernel,
        [((half_rows, lanes, chans), F32)] * 3,
        *near_pieces, query, bias,
        room=24 * MIB,
    )
    keep, send = vmem_call(
        far_kernel,
        [((half_rows, width, chans), BF16)] * 2,
        *far_pieces, query, bias, *state, gate, w_kv, w_out,
        room=24 * MIB,
        scratch=[
            pltpu.VMEM((HEADS, half_rows, cols, chans), BF16),
            pltpu.VMEM((half_rows, cols, chans), BF16),
        ],
    )
    return vmem_call(join_kernel, [(pair.shape, BF16)], keep, swap_core(send), in_hbm=True)


def travel(n_dev):
    chips = n_dev // 2
    far_bits = [4 << k for k in range((chips // 4).bit_length() - 1)]
    return far_bits, far_bits[:-1] + ["first", "second"] + far_bits[-1:]


def solution(mesh):
    n_dev = mesh.shape["col"]
    in_specs = (P("grp", "col", None), P(), P(), P(), P(), P("grp", "col", None), P("grp"))
    out_specs = P("grp", "col", None)

    def body(*args):
        return on_device(n_dev, *args)

    return jax.shard_map(
        body, mesh=mesh, in_specs=in_specs, out_specs=out_specs, check_vma=False
    )
```

```python
import functools
import math

import jax
import jax.numpy as jnp
from jax import lax
from jax.experimental import pallas as pl
from jax.experimental.pallas import tpu as pltpu
from jax.sharding import PartitionSpec as P


HEADS = 4
F32 = jnp.float32
BF16 = jnp.bfloat16
MIB = 1 << 20
FIRST, SECOND = 0, 1
LOG2_E = math.log2(math.e)


def vmem_call(kernel, outs, *args, plain=(), in_hbm=False, scratch=(), scalars=(), room=4 * MIB):
    args = [pltpu.with_memory_space_constraint(a, pltpu.VMEM) for a in args]
    plain = [pltpu.with_memory_space_constraint(a, pltpu.HBM) for a in plain]
    if in_hbm:
        out_shape = [jax.ShapeDtypeStruct(*o) for o in outs]
    else:
        out_shape = [pltpu.VMEM(*o) for o in outs]
    call = pl.pallas_call(
        kernel,
        in_specs=[pl.BlockSpec(memory_space=pltpu.SMEM)] * len(scalars)
        + [pl.BlockSpec(memory_space=pl.ANY)] * len(plain)
        + [pl.BlockSpec(memory_space=pltpu.VMEM)] * len(args),
        out_specs=[pl.BlockSpec(memory_space=pltpu.VMEM)] * len(outs),
        out_shape=out_shape,
        scratch_shapes=scratch,
        compiler_params=pltpu.CompilerParams(vmem_limit_bytes=room),
    )
    results = call(*scalars, *plain, *args)
    return results if len(outs) > 1 else results[0]


def my_place():
    index = lax.axis_index("col")
    return index >> 1, index & 1


def by_core(core, on_first, on_second):
    return on_first + core * (on_second - on_first)


def contract_last(a, b):
    return lax.dot_general(a, b, (((1,), (1,)), ((), ())), preferred_element_type=F32)


def normalized(values):
    values_f = values.astype(F32)
    mean_val = jnp.mean(values_f, axis=-1, keepdims=True)
    centred = values_f - mean_val
    variance = jnp.mean(centred * centred, axis=-1, keepdims=True)
    return (centred * lax.rsqrt(variance + 1e-05)).astype(BF16)


def early_kernel(
    dims, stages, pair_hbm, bias_hbm, own_ref, keep_ref, send_ref, packed_ref, pair_ref, bias_ref, sems
):
    half_rows = own_ref.shape[0]
    _, core = my_place()
    pair_copy = pltpu.make_async_copy(
        pair_hbm.at[pl.ds(core * half_rows, half_rows)], pair_ref, sems.at[0]
    )
    bias_copy = pltpu.make_async_copy(bias_hbm, bias_ref, sems.at[1])
    pair_copy.start()
    bias_copy.start()
    pair_copy.wait()
    own_ref[...] = normalized(pair_ref[...])
    bias_copy.wait()
    pack_bias(dims, stages, bias_ref, keep_ref, send_ref, packed_ref)


def norm_kernel(own_ref, other_ref, block_ref):
    half_rows, width, _ = own_ref.shape
    _, core = my_place()
    own_at = pl.multiple_of(core * width, width)
    other_at = pl.multiple_of((1 - core) * width, width)
    block_ref[0, :, pl.ds(own_at, width), :] = own_ref[...]
    block_ref[0, :, pl.ds(other_at, width), :] = normalized(
        other_ref[pl.ds(core * half_rows, half_rows)]
    )


def stack_kernel(first_ref, second_ref, out_ref):
    count = first_ref.shape[0]
    out_ref[:count] = first_ref[...]
    out_ref[count:] = second_ref[...]


def query_kernel(block_ref, w_query_ref, w_kv_ref, w_gate_ref, query_ref, gate_ref):
    _, rows, cols, chans = block_ref.shape
    head_width = chans // HEADS
    tokens = block_ref[...].reshape(rows * cols, chans)
    queries = (
        jnp.dot(tokens, w_query_ref[...], preferred_element_type=F32) * head_width ** (-0.5)
    ).astype(BF16)
    lane_head = lax.broadcasted_iota(jnp.int32, queries.shape, 1) // head_width
    w_key = w_kv_ref[:, :chans]
    for head in range(HEADS):
        masked = jnp.where(lane_head == head, queries, jnp.zeros_like(queries))
        back = (contract_last(masked, w_key) * LOG2_E).astype(BF16)
        query_ref[:, head * cols : (head + 1) * cols, :] = back.reshape(rows, cols, chans)
    gate = jax.nn.sigmoid(jnp.dot(tokens, w_gate_ref[...], preferred_element_type=F32))
    gate_ref[...] = gate.reshape(rows, cols, chans)


def pack_bias(dims, stages, bias_ref, keep_ref, send_ref, packed_ref):
    half = keep_ref.shape[1]
    chips, _, lanes = packed_ref.shape
    cols = lanes // HEADS
    chip, core = my_place()
    shifts = [by_core(core, *(bit.bit_length() - 1 for bit in dims[stage])) for stage in stages]
    for target in range(chips):
        apart = chip ^ target
        spot = 0
        for shift in shifts:
            spot = spot * 2 + ((apart >> shift) & 1)
        for head in range(HEADS):
            packed_ref[spot, :, head * cols : (head + 1) * cols] = bias_ref[
                head, :, target * cols : (target + 1) * cols
            ]
    keep_ref[0] = packed_ref[:half]
    send_ref[0] = packed_ref[half:]


def trade_kernel(keep_ref, recv_ref, next_keep_ref, next_send_ref):
    sources, targets = keep_ref.shape[:2]
    half = targets // 2
    next_keep_ref[:sources] = keep_ref[:, :half]
    next_keep_ref[sources:] = recv_ref[:, :half]
    next_send_ref[:sources] = keep_ref[:, half:]
    next_send_ref[sources:] = recv_ref[:, half:]


def bias_kernel(dims, offsets, held_at, limit_ref, own_a, own_b, other_a, other_b, bias_ref, keys_ref):
    sources, _, width, lanes = own_a.shape
    chip, core = my_place()
    limit = limit_ref[0]
    apart = [by_core(core, *pair) for pair in dims]
    row_at = lax.broadcasted_iota(jnp.int32, (width, lanes), 0)
    for spot, taken in enumerate(offsets):
        source = chip
        for dim in taken:
            source = source ^ apart[dim]
        mirrored = frozenset(dims.index(dims[dim][::-1]) for dim in taken)
        for parts, part, seen in (
            ((own_a, own_b), core, taken),
            ((other_a, other_b), 1 - core, mirrored),
        ):
            first_key = (source * 2 + part) * width
            mask = jnp.where(first_key + row_at < limit, 0.0, -1000000000.0).astype(F32)
            at = pl.multiple_of(spot * 2 * width + part * width, width)
            held = held_at[seen]
            value = parts[held // sources][held % sources, 0]
            keys_ref[pl.ds(at, width), :] = (value.astype(F32) + mask) * LOG2_E
    bias_ref[...] = keys_ref[...].T


def attend_rows(key_at, pieces, query_ref, bias_ref, finish):
    rows, lanes, chans = query_ref.shape
    n_keys = sum(piece.shape[0] * piece.shape[2] for piece in pieces)
    step = rows
    while step > 1 and step * lanes * n_keys * 4 > 4 * MIB:
        step //= 2

    def advance(turn, carry):
        at = [turn * step + inner for inner in range(step)]
        keys = [
            jnp.concatenate([piece[:, row].reshape(-1, chans) for piece in pieces], axis=0)
            for row in at
        ]
        bias = bias_ref[:, key_at : key_at + n_keys]
        scores = [contract_last(query_ref[row], key) + bias for row, key in zip(at, keys)]
        tops = [jnp.max(score, axis=-1, keepdims=True) for score in scores]
        expons = [jnp.exp2(score - top) for score, top in zip(scores, tops)]
        totals = [jnp.sum(expon, axis=-1, keepdims=True) for expon in expons]
        mixes = [
            jnp.dot(expon.astype(BF16), key, preferred_element_type=F32)
            for expon, key in zip(expons, keys)
        ]
        for values in zip(at, tops, totals, mixes):
            finish(*values)
        return carry

    if step == rows:
        advance(0, 0)
    else:
        lax.fori_loop(0, rows // step, advance, 0)


def near_kernel(*refs):
    pieces = refs[:-5]
    query_ref, bias_ref, top_ref, total_ref, mixed_ref = refs[-5:]

    def finish(row, top, total, mixed):
        top_ref[row] = jnp.broadcast_to(top, mixed.shape)
        total_ref[row] = jnp.broadcast_to(total, mixed.shape)
        mixed_ref[row] = mixed

    attend_rows(0, pieces, query_ref, bias_ref, finish)


def far_kernel(*refs):
    pieces = refs[:4]
    (query_ref, bias_ref, top_ref, total_ref, mixed_ref, gate_ref, w_kv_ref, w_out_ref) = refs[4:12]
    keep_ref, send_ref, ready_ref, out_ref = refs[12:]
    rows, cols, chans = gate_ref.shape
    width = keep_ref.shape[1]
    head_width = chans // HEADS
    half_keys = bias_ref.shape[1] // 2

    def finish(row, top, total, mixed):
        old_top = top_ref[row]
        new_top = jnp.maximum(old_top, top)
        old_scale = jnp.exp2(old_top - new_top)
        scale = jnp.exp2(top - new_top)
        inverse = 1.0 / (total_ref[row] * old_scale + total * scale)
        both = mixed_ref[row] * (old_scale * inverse) + mixed * (scale * inverse)
        both = both.astype(BF16)
        for head in range(HEADS):
            ready_ref[head, row] = both[head * cols : (head + 1) * cols]

    attend_rows(half_keys, pieces, query_ref, bias_ref, finish)

    w_value = w_kv_ref[:, chans:]
    lane_head = lax.broadcasted_iota(jnp.int32, w_value.shape, 1) // head_width
    values = [jnp.where(lane_head == h, w_value, jnp.zeros_like(w_value)) for h in range(HEADS)]
    ready = [ready_ref[h].reshape(rows * cols, chans) for h in range(HEADS)]
    attended = jnp.dot(
        jnp.concatenate(ready, axis=1), jnp.concatenate(values, axis=0), preferred_element_type=F32
    )
    hidden = (gate_ref[...].reshape(rows * cols, chans) * attended).astype(BF16)
    update = jnp.dot(hidden, w_out_ref[...], preferred_element_type=F32).astype(BF16)
    out_ref[...] = update.reshape(rows, cols, chans)
    _, core = my_place()
    keep_ref[...] = out_ref[:, pl.ds(pl.multiple_of(core * width, width), width), :]
    send_ref[...] = out_ref[:, pl.ds(pl.multiple_of((1 - core) * width, width), width), :]


def join_kernel(keep_ref, recv_ref, out_ref):
    half_rows = keep_ref.shape[0]
    _, core = my_place()
    out_ref[pl.ds(core * half_rows, half_rows)] = keep_ref[...]
    out_ref[pl.ds((1 - core) * half_rows, half_rows)] = recv_ref[...]


def on_device(n_dev, pair, w_query, w_kv, w_gate, w_out, pair_bias, lengths):
    rows, width, chans = pair.shape
    half_rows = rows // 2
    cols = 2 * width
    lanes = HEADS * cols
    chips = n_dev // 2

    def swap(value, dim):
        perm = [(d, ((d // 2) ^ dims[dim][d % 2]) * 2 + d % 2) for d in range(n_dev)]
        return lax.ppermute(value, "col", perm)

    def swap_core(value):
        return lax.ppermute(value, "col", [(d, d ^ 1) for d in range(n_dev)])

    def stack(first, second):
        shape = (first.shape[0] + second.shape[0],) + first.shape[1:]
        return vmem_call(stack_kernel, [(shape, BF16)], first, second)

    def spread(piece, offsets):
        first = swap(piece, FIRST)
        second = swap(stack(piece, first), SECOND)
        return [piece, first, second], plane(offsets)

    def spread_apart(piece, offsets):
        first = swap(piece, FIRST)
        second = swap(piece, SECOND)
        third = swap(first, SECOND)
        return [piece, first, second, third], plane(offsets)

    def plane(offsets):
        steps = ((), (FIRST,), (SECOND,), (FIRST, SECOND))
        return [taken.union(step) for step in steps for taken in offsets]

    dims, stages = travel(n_dev)
    far_dims = range(2, len(dims))

    other = swap_core(pair)
    half_targets = ((1, chips // 2, width, lanes), BF16)
    own, keep_bias, send_bias = vmem_call(
        functools.partial(early_kernel, dims, stages),
        [((half_rows, width, chans), BF16), half_targets, half_targets],
        plain=[pair, pair_bias],
        scratch=[
            pltpu.VMEM((chips, width, lanes), BF16),
            pltpu.VMEM((half_rows, width, chans), BF16),
            pltpu.VMEM(pair_bias.shape, BF16),
            pltpu.SemaphoreType.DMA((2,)),
        ],
        room=4 * MIB + 8 * chips * width * lanes,
    )
    near = vmem_call(norm_kernel, [((1, half_rows, cols, chans), BF16)], own, other)
    block = near

    near_offsets = [frozenset()]
    near_pieces, offsets = spread(block, near_offsets)
    for dim in far_dims[:-1]:
        arrived = swap(near, dim)
        near = stack(near, arrived)
        arrived_offsets = [taken | {dim} for taken in near_offsets]
        pieces, order = spread(arrived, arrived_offsets)
        near_pieces, offsets = near_pieces + pieces, offsets + order
        near_offsets = near_offsets + arrived_offsets
    far = swap(near, far_dims[-1])
    far_pieces, order = spread_apart(far, [taken | {far_dims[-1]} for taken in near_offsets])
    offsets = offsets + order

    for stage in stages[:-1]:
        recv_bias = swap(send_bias, stage)
        sources, targets = keep_bias.shape[:2]
        shape = (2 * sources, targets // 2, width, lanes)
        keep_bias, send_bias = vmem_call(trade_kernel, [(shape, BF16)] * 2, keep_bias, recv_bias)
    recv_bias = swap(send_bias, stages[-1])
    held_at = {
        frozenset(dim for k, dim in enumerate(stages) if held >> k & 1): held
        for held in range(chips)
    }

    query, gate = vmem_call(
        query_kernel,
        [((half_rows, lanes, chans), BF16), ((half_rows, cols, chans), F32)],
        block, w_query, w_kv, w_gate,
    )
    n_keys = chips * cols
    bias = vmem_call(
        functools.partial(bias_kernel, dims, offsets, held_at),
        [((lanes, n_keys), F32)],
        keep_bias, recv_bias,
        swap_core(keep_bias), swap_core(recv_bias),
        scratch=[pltpu.VMEM((n_keys, lanes), F32)],
        scalars=[lengths],
        room=4 * MIB + 3 * n_keys * lanes * 4,
    )
    state = vmem_call(
        near_kernel,
        [((half_rows, lanes, chans), F32)] * 3,
        *near_pieces, query, bias,
        room=24 * MIB,
    )
    keep, send = vmem_call(
        far_kernel,
        [((half_rows, width, chans), BF16)] * 2,
        *far_pieces, query, bias, *state, gate, w_kv, w_out,
        room=24 * MIB,
        scratch=[
            pltpu.VMEM((HEADS, half_rows, cols, chans), BF16),
            pltpu.VMEM((half_rows, cols, chans), BF16),
        ],
    )
    return vmem_call(join_kernel, [(pair.shape, BF16)], keep, swap_core(send), in_hbm=True)


def travel(n_dev):
    chips = n_dev // 2
    far_bits = [4 << k for k in range((chips // 4).bit_length() - 1)]
    dims = [(1, 2), (2, 1)] + list(zip(far_bits[::-1], far_bits))
    return dims, list(range(len(dims)))


def solution(mesh):
    n_dev = mesh.shape["col"]
    in_specs = (P("grp", "col", None), P(), P(), P(), P(), P("grp", "col", None), P("grp"))
    out_specs = P("grp", "col", None)

    def body(*args):
        return on_device(n_dev, *args)

    return jax.shard_map(
        body, mesh=mesh, in_specs=in_specs, out_specs=out_specs, check_vma=False
    )
```
